32 devices in a mesh: groups: 2 (over y), blk: 4 (over z), rep: 2 (over x), sub: 2 (over core).
Axes of the slice: x: 2, y: 2, z: 4, core: 2. Of those that a mesh axis runs over, the one named last changes fastest.
Arguments:
- replica_delta: bfloat16 [32, 32, 4608], P(('groups', 'blk', 'rep', 'sub')), parts along dimension 0, may hold values from -150 to 150
- momentum: float32 [64, 4608], P(('groups', 'blk')), parts along dimension 0, may hold values from -6 to 6
- params: float32 [64, 4608], P(('groups', 'blk')), parts along dimension 0, may hold values from -6 to 6
- prev_master: float32 [64, 4608], P(('groups', 'blk')), parts along dimension 0, may hold values from -6 to 6
Outputs:
- new_params: float32 [64, 4608], P(('groups', 'blk')), parts along dimension 0
- new_momentum: float32 [64, 4608], P(('groups', 'blk')), parts along dimension 0
- prev_weights: bfloat16 [64, 4608], P('groups'), parts along dimension 0
The draws below stay inside these ranges and needn't reach their ends.
There are 2 independent parts, one for each index of `groups`. The reference program is written for one: setup_inputs(seed, part) draws one part's arguments, and reference() takes and returns one part's arrays. A program takes and returns all parts, laid end to end along the dimension named above; each array names one. Nothing has to cross between parts.
All inputs are finite; a program needn't handle non-finite values.
Results may differ from the reference program's by a relative error of at most 0.012.
Values may be sent and summed in bfloat16 or wider, within the bound.
A program may use at most 64 MiB of HBM per device.

```python
import math
import jax
import jax.numpy as jnp
from jax import lax

D = 4608
ROW_OWN = 8
LROWS = 32
REPLICAS = 16


def draw_replica_delta(key, part):
    base_key = jax.random.fold_in(key, 11)
    key_rows, key_cols, key_noise, key_shared, key_blocks = jax.random.split(base_key, 5)
    trend = jnp.power(3.0, jnp.arange(LROWS, dtype=jnp.float32) / max(LROWS - 1, 1))
    row_scale = jnp.exp(jax.random.uniform(key_rows, (LROWS,), jnp.float32) * math.log(10.0)) * trend
    col_scale = jnp.exp(jax.random.uniform(key_cols, (D,), jnp.float32) * math.log(10.0))
    block_count = LROWS // ROW_OWN
    chosen = jax.random.permutation(key_blocks, block_count) < block_count // 2
    indep = jax.random.normal(key_noise, (REPLICAS, LROWS, D), jnp.float32)
    shared = jax.random.normal(key_shared, (1, LROWS, D), jnp.float32)
    target = 9.0
    rho_square = min(target / max(REPLICAS - 1, 1), 0.9)
    block_rho = jnp.where(chosen, jnp.float32(math.sqrt(rho_square)), jnp.float32(0.0))
    row_rho = jnp.repeat(block_rho, ROW_OWN)[None, :, None]
    noise = row_rho * shared + jnp.sqrt(1.0 - row_rho * row_rho) * indep
    noise = jnp.clip(noise, -4.0, 4.0)
    values = noise * row_scale[None, :, None] * col_scale[None, None, :] / 8.0
    return values.astype(jnp.bfloat16)


def levels(own_key, dims, pieces, low, high):
    def one(dim, parts):
        draws = jax.random.uniform(jax.random.fold_in(jax.random.fold_in(own_key, 6), dim), (parts,), jnp.float32, low / len(pieces), high / len(pieces))
        return jnp.repeat(jnp.exp(draws), dims[dim] // parts).reshape((-1,) + (1,) * (len(dims) - dim - 1))

    factor_of = one(*pieces[0])
    for cut in pieces[1:]:
        factor_of = factor_of * one(*cut)
    return factor_of


def gaussian(stream_key, extent, deviation, limit, shards=(), held_as=jnp.bfloat16):
    result = deviation * jax.random.normal(stream_key, extent, jnp.float32)
    if shards:
        result = result * levels(stream_key, extent, shards, -0.22, 0.18)
    return jnp.clip(result, -limit, limit).astype(held_as)


def setup_inputs(seed: int = 0, part: int = 0) -> dict:
    keys = jax.random.split(jax.random.key(seed), 5)
    part_splits = jax.random.split(jax.random.fold_in(keys[4], part), 5)
    return {
        "replica_delta": draw_replica_delta(jax.random.fold_in(jax.random.fold_in(keys[4], part), 71), part),
        "momentum": gaussian(part_splits[1], (LROWS, D), 1.0, 6.0, ((0, 4),), jnp.float32),
        "params": gaussian(part_splits[2], (LROWS, D), 1.0, 6.0, ((0, 4),), jnp.float32),
        "prev_master": gaussian(part_splits[3], (LROWS, D), 1.0, 6.0, ((0, 4),), jnp.float32),
    }


momentum_coef = 0.9
outer_rate = 0.7

def reference(replica_delta, momentum, params, prev_master):
    summed = lax.optimization_barrier(jnp.sum(replica_delta, axis=0, dtype=jnp.float32))
    squares = jnp.sum(summed * summed)
    entries = replica_delta.shape[1] * replica_delta.shape[2]
    clip_factor = jnp.minimum(jnp.float32(1.0), jnp.sqrt(jnp.float32(entries)) / jnp.sqrt(squares + 1e-06))
    scaled = clip_factor * summed
    new_momentum = momentum_coef * momentum + scaled
    new_params = params - outer_rate * (scaled + momentum_coef * new_momentum)
    prev_weights = prev_master.astype(jnp.bfloat16)
    return (new_params, new_momentum, prev_weights)
```

```python
import functools
import itertools
import math

import jax
import jax.numpy as jnp
from jax import lax
from jax.experimental import pallas as pl
from jax.experimental.pallas import tpu as pltpu
from jax.sharding import PartitionSpec as P

momentum_coef = 0.9
outer_rate = 0.7
MESH = pl.DeviceIdType.MESH
LANES = 128


def flip(index, mask):
    bit = 1
    while bit <= mask:
        if mask & bit:
            index = index + bit * (1 - 2 * ((index // bit) % 2))
        bit *= 2
    return index


def kernel(sizes, delta_hbm, mom_hbm, par_hbm, prev_hbm, new_par_hbm, new_mom_hbm, prev_out_hbm,
           delta, mom, par, prev, recv1, half, mine, recv2, part, recv3, total, squares, weights, new_par, new_mom,
           load_sem, store_sem, send1, got1, send2, got2, send3, got3, send_g, got_g, send_q, got_q,
           send_pz, got_pz, send_px, got_px, send_pc, got_pc):
    nz, nx, ns = sizes
    z, x, s = lax.axis_index("blk"), lax.axis_index("rep"), lax.axis_index("sub")
    own, width = mom.shape
    half_width = width // ns
    piece = half_width // nx

    def columns(core, rep):
        return pl.ds(pl.multiple_of(core * half_width + rep * piece, LANES), piece)

    def half_columns(core):
        return pl.ds(pl.multiple_of(core * half_width, LANES), half_width)

    def inner(rep):
        return pl.ds(pl.multiple_of(rep * piece, LANES), piece)

    def peer(tz, tx, ts):
        return {"blk": flip(z, tz), "rep": flip(x, tx), "sub": flip(s, ts)}

    def remote(src, dst, send, got, to):
        copy = pltpu.make_async_remote_copy(
            src_ref=src, dst_ref=dst, send_sem=send, recv_sem=got, device_id=peer(*to), device_id_type=MESH
        )
        copy.start()
        started.append(copy)
        return copy

    started = []
    offsets = [o for o in itertools.product(range(nz), range(nx), range(ns)) if o != (0, 0, 0)]
    barrier = pltpu.get_barrier_semaphore()
    for o in offsets:
        pl.semaphore_signal(barrier, inc=1, device_id=peer(*o), device_id_type=MESH)

    loads = [
        pltpu.make_async_copy(src, dst, load_sem.at[i])
        for i, (src, dst) in enumerate(((prev_hbm, prev), (delta_hbm, delta), (mom_hbm, mom), (par_hbm, par)))
    ]
    for copy in loads:
        copy.start()
    loads[0].wait()
    weights[z] = prev[...].astype(weights.dtype)
    loads[1].wait()
    pl.semaphore_wait(barrier, len(offsets))

    order = list(range(nz - 1, -1, -1))
    first = {
        t: remote(delta.at[flip(z, t), :, half_columns(1 - s)], recv1.at[t], send1.at[t], got1.at[t], (0, 0, 1))
        for t in order
    }
    across = {
        t: remote(weights.at[z, :, columns(s, x)], weights.at[z, :, columns(s, x)], send_pz.at[t], got_pz.at[t], (t, 0, 0))
        for t in order if t
    }

    second, third = {}, {}

    def stage_two(t):
        first[t].wait_recv()
        zt = flip(z, t)
        for u in range(nx - 1, 0, -1):
            xu = flip(x, u)
            half[t, u] = (
                delta[zt, :, columns(s, xu)].astype(jnp.float32) + recv1[t, :, inner(xu)].astype(jnp.float32)
            ).astype(half.dtype)
            second[t, u] = remote(half.at[t, u], recv2.at[t, u], send2.at[t, u], got2.at[t, u], (0, u, 0))
        mine[t] = delta[zt, :, columns(s, x)].astype(jnp.float32) + recv1[t, :, inner(x)].astype(jnp.float32)

    def stage_three(t):
        value = mine[t]
        for u in range(1, nx):
            second[t, u].wait_recv()
            value = value + recv2[t, u].astype(jnp.float32)
        if t:
            part[t] = value.astype(part.dtype)
            third[t] = remote(part.at[t], recv3.at[t], send3.at[t], got3.at[t], (t, 0, 0))
        else:
            mine[t] = value

    for i, t in enumerate(order):
        stage_two(t)
        if i:
            stage_three(order[i - 1])
    stage_three(order[-1])

    along = {}
    for t in order:
        if t:
            across[t].wait_recv()
            place = weights.at[flip(z, t), :, columns(s, x)]
            for u in range(1, nx):
                along[t, u] = remote(place, place, send_px.at[t, u], got_px.at[t, u], (0, u, 0))

    value = mine[0]
    for t in sorted(third):
        third[t].wait_recv()
        value = value + recv3[t].astype(jnp.float32)
    rounded = value.astype(total.dtype)
    total[:, columns(s, x)] = rounded
    value = rounded.astype(jnp.float32)
    square = jnp.sum(value * value, axis=0, keepdims=True)
    lanes = square[:, :LANES]
    for c in range(1, piece // LANES):
        lanes = lanes + square[:, c * LANES : (c + 1) * LANES]
    place = (z * nx + x) * ns + s
    squares[place] = lanes
    norms = [
        remote(squares.at[place], squares.at[place], send_q.at[i], got_q.at[i], o)
        for i, o in sorted(enumerate(offsets), key=lambda e: (-e[1][0], -e[1][1], -e[1][2]))
    ]
    sums = [
        remote(total.at[:, columns(s, x)], total.at[:, columns(s, x)], send_g.at[u, c], got_g.at[u, c], (0, u, c))
        for u in range(nx - 1, -1, -1) for c in range(ns - 1, -1, -1) if u or c
    ]

    over = {}
    for t in order:
        if t:
            for u in range(1, nx):
                along[t, u].wait_recv()
            place = weights.at[flip(z, t), :, half_columns(s)]
            over[t] = remote(place, place, send_pc.at[t], got_pc.at[t], (0, 0, 1))

    loads[2].wait()
    loads[3].wait()
    for copy in sums:
        copy.wait_recv()
    for t in over:
        over[t].wait_recv()
    stores = [pltpu.make_async_copy(weights, prev_out_hbm, store_sem.at[0])]
    stores[0].start()
    for copy in norms:
        copy.wait_recv()
    norm = jnp.sum(jnp.sum(squares[...], axis=0), axis=1, keepdims=True)
    limit = math.sqrt(nz * own * width)
    clip = jnp.minimum(jnp.float32(1.0), jnp.float32(limit) / jnp.sqrt(norm + jnp.float32(1e-06)))
    scaled = clip * total[...].astype(jnp.float32)
    fresh = momentum_coef * mom[...] + scaled
    new_mom[...] = fresh
    stores.append(pltpu.make_async_copy(new_mom, new_mom_hbm, store_sem.at[1]))
    stores[-1].start()
    new_par[...] = par[...] - outer_rate * (scaled + momentum_coef * fresh)
    stores.append(pltpu.make_async_copy(new_par, new_par_hbm, store_sem.at[2]))
    stores[-1].start()
    for copy in started:
        copy.wait_send()
    for copy in stores:
        copy.wait()


def by_kernel(sizes, replica_delta, momentum, params, prev_master):
    nz, nx, ns = sizes
    own, width = momentum.shape
    half, piece = width // ns, width // (ns * nx)
    b16, f32, dma = jnp.bfloat16, jnp.float32, pltpu.SemaphoreType.DMA
    delta = replica_delta.reshape(nz, own, width)
    any_space = pl.BlockSpec(memory_space=pl.ANY)
    new_params, new_momentum, weights = pl.pallas_call(
        functools.partial(kernel, sizes),
        out_shape=(
            jax.ShapeDtypeStruct((own, width), f32),
            jax.ShapeDtypeStruct((own, width), f32),
            jax.ShapeDtypeStruct((nz, own, width), b16),
        ),
        in_specs=[any_space] * 4,
        out_specs=[any_space] * 3,
        scratch_shapes=[
            pltpu.VMEM((nz, own, width), b16),
            pltpu.VMEM((own, width), f32),
            pltpu.VMEM((own, width), f32),
            pltpu.VMEM((own, width), f32),
            pltpu.VMEM((nz, own, half), b16),
            pltpu.VMEM((nz, nx, own, piece), b16),
            pltpu.VMEM((nz, own, piece), f32),
            pltpu.VMEM((nz, nx, own, piece), b16),
            pltpu.VMEM((nz, own, piece), b16),
            pltpu.VMEM((nz, own, piece), b16),
            pltpu.VMEM((own, width), b16),
            pltpu.VMEM((nz * nx * ns, 1, LANES), f32),
            pltpu.VMEM((nz, own, width), b16),
            pltpu.VMEM((own, width), f32),
            pltpu.VMEM((own, width), f32),
            dma((4,)), dma((3,)),
            dma((nz,)), dma((nz,)),
            dma((nz, nx)), dma((nz, nx)),
            dma((nz,)), dma((nz,)),
            dma((nx, ns)), dma((nx, ns)),
            dma((nz * nx * ns,)), dma((nz * nx * ns,)),
            dma((nz,)), dma((nz,)),
            dma((nz, nx)), dma((nz, nx)),
            dma((nz,)), dma((nz,)),
        ],
        compiler_params=pltpu.CompilerParams(collective_id=0, has_side_effects=True),
    )(delta, momentum, params, prev_master)
    return new_params, new_momentum, weights.reshape(nz * own, width)


def by_collectives(replica_delta, momentum, params, prev_master):
    own_delta = replica_delta[0]
    entries = own_delta.shape[0] * own_delta.shape[1]
    share_sum = lax.psum_scatter(own_delta, "blk", scatter_dimension=0, tiled=True)
    summed = lax.psum(share_sum, ("rep", "sub")).astype(jnp.float32)
    squares = lax.psum(jnp.sum(summed * summed), "blk")
    clip_factor = jnp.minimum(
        jnp.float32(1.0), jnp.sqrt(jnp.float32(entries)) / jnp.sqrt(squares + 1e-06)
    )
    scaled = clip_factor * summed
    new_momentum = momentum_coef * momentum + scaled
    new_params = params - outer_rate * (scaled + momentum_coef * new_momentum)
    prev_weights = lax.all_gather(prev_master.astype(jnp.bfloat16), "blk", axis=0, tiled=True)
    return (new_params, new_momentum, prev_weights)


def solution(mesh):
    sizes = tuple(mesh.shape[a] for a in ("blk", "rep", "sub"))

    def per_device(replica_delta, momentum, params, prev_master):
        width = momentum.shape[1]
        whole_pieces = width % (LANES * sizes[1] * sizes[2]) == 0
        powers = all(n & (n - 1) == 0 for n in sizes) and sizes[2] == 2
        if whole_pieces and powers:
            return by_kernel(sizes, replica_delta, momentum, params, prev_master)
        return by_collectives(replica_delta, momentum, params, prev_master)

    in_specs = (
        P(("groups", "blk", "rep", "sub"), None, None),
        P(("groups", "blk"), None),
        P(("groups", "blk"), None),
        P(("groups", "blk"), None),
    )
    out_specs = (P(("groups", "blk"), None), P(("groups", "blk"), None), P("groups", None))
    return jax.shard_map(
        per_device, mesh=mesh, in_specs=in_specs, out_specs=out_specs, check_vma=False
    )
```

```python
import functools
import itertools
import math

import jax
import jax.numpy as jnp
from jax import lax
from jax.experimental import pallas as pl
from jax.experimental.pallas import tpu as pltpu
from jax.sharding import PartitionSpec as P

momentum_coef = 0.9
outer_rate = 0.7
MESH = pl.DeviceIdType.MESH
LANES = 128


def flip(index, mask):
    bit = 1
    while bit <= mask:
        if mask & bit:
            index = index + bit * (1 - 2 * ((index // bit) % 2))
        bit *= 2
    return index


def exchange(sizes, delta_hbm, mom_hbm, par_hbm, prev_hbm, total, squares, weights, mom, par,
             delta, prev, recv1, half, mine, recv2, part, recv3,
             load_sem, send1, got1, send2, got2, send3, got3, send_g, got_g, send_q, got_q,
             send_pz, got_pz, send_px, got_px, send_pc, got_pc):
    nz, nx, ns = sizes
    z, x, s = lax.axis_index("blk"), lax.axis_index("rep"), lax.axis_index("sub")
    own, width = mom.shape
    half_width = width // ns
    piece = half_width // nx

    def columns(core, rep):
        return pl.ds(pl.multiple_of(core * half_width + rep * piece, LANES), piece)

    def half_columns(core):
        return pl.ds(pl.multiple_of(core * half_width, LANES), half_width)

    def inner(rep):
        return pl.ds(pl.multiple_of(rep * piece, LANES), piece)

    def peer(tz, tx, ts):
        return {"blk": flip(z, tz), "rep": flip(x, tx), "sub": flip(s, ts)}

    def remote(src, dst, send, got, to):
        copy = pltpu.make_async_remote_copy(
            src_ref=src, dst_ref=dst, send_sem=send, recv_sem=got, device_id=peer(*to), device_id_type=MESH
        )
        copy.start()
        started.append(copy)
        return copy

    started = []
    offsets = [o for o in itertools.product(range(nz), range(nx), range(ns)) if o != (0, 0, 0)]
    barrier = pltpu.get_barrier_semaphore()
    for o in offsets:
        pl.semaphore_signal(barrier, inc=1, device_id=peer(*o), device_id_type=MESH)

    loads = [
        pltpu.make_async_copy(src, dst, load_sem.at[i])
        for i, (src, dst) in enumerate(((prev_hbm, prev), (delta_hbm, delta), (mom_hbm, mom), (par_hbm, par)))
    ]
    for copy in loads:
        copy.start()
    loads[0].wait()
    weights[z] = prev[...].astype(weights.dtype)
    loads[1].wait()
    pl.semaphore_wait(barrier, len(offsets))

    order = list(range(nz - 1, -1, -1))
    first = {
        t: remote(delta.at[flip(z, t), :, half_columns(1 - s)], recv1.at[t], send1.at[t], got1.at[t], (0, 0, 1))
        for t in order
    }
    across = {
        t: remote(weights.at[z, :, columns(s, x)], weights.at[z, :, columns(s, x)], send_pz.at[t], got_pz.at[t], (t, 0, 0))
        for t in order if t
    }

    second, third = {}, {}

    def stage_two(t):
        first[t].wait_recv()
        zt = flip(z, t)
        for u in range(nx - 1, 0, -1):
            xu = flip(x, u)
            half[t, u] = (
                delta[zt, :, columns(s, xu)].astype(jnp.float32) + recv1[t, :, inner(xu)].astype(jnp.float32)
            ).astype(half.dtype)
            second[t, u] = remote(half.at[t, u], recv2.at[t, u], send2.at[t, u], got2.at[t, u], (0, u, 0))
        mine[t] = delta[zt, :, columns(s, x)].astype(jnp.float32) + recv1[t, :, inner(x)].astype(jnp.float32)

    def stage_three(t):
        value = mine[t]
        for u in range(1, nx):
            second[t, u].wait_recv()
            value = value + recv2[t, u].astype(jnp.float32)
        if t:
            part[t] = value.astype(part.dtype)
            third[t] = remote(part.at[t], recv3.at[t], send3.at[t], got3.at[t], (t, 0, 0))
        else:
            mine[t] = value

    for i, t in enumerate(order):
        stage_two(t)
        if i:
            stage_three(order[i - 1])
    stage_three(order[-1])

    along = {}
    for t in order:
        if t:
            across[t].wait_recv()
            place = weights.at[flip(z, t), :, columns(s, x)]
            for u in range(1, nx):
                along[t, u] = remote(place, place, send_px.at[t, u], got_px.at[t, u], (0, u, 0))

    value = mine[0]
    for t in sorted(third):
        third[t].wait_recv()
        value = value + recv3[t].astype(jnp.float32)
    rounded = value.astype(total.dtype)
    total[:, columns(s, x)] = rounded
    value = rounded.astype(jnp.float32)
    square = jnp.sum(value * value, axis=0, keepdims=True)
    lanes = square[:, :LANES]
    for c in range(1, piece // LANES):
        lanes = lanes + square[:, c * LANES : (c + 1) * LANES]
    place = (z * nx + x) * ns + s
    squares[place] = lanes
    norms = [
        remote(squares.at[place], squares.at[place], send_q.at[i], got_q.at[i], o)
        for i, o in sorted(enumerate(offsets), key=lambda e: (-e[1][0], -e[1][1], -e[1][2]))
    ]
    sums = [
        remote(total.at[:, columns(s, x)], total.at[:, columns(s, x)], send_g.at[u, c], got_g.at[u, c], (0, u, c))
        for u in range(nx - 1, -1, -1) for c in range(ns - 1, -1, -1) if u or c
    ]

    over = {}
    for t in order:
        if t:
            for u in range(1, nx):
                along[t, u].wait_recv()
            place = weights.at[flip(z, t), :, half_columns(s)]
            over[t] = remote(place, place, send_pc.at[t], got_pc.at[t], (0, 0, 1))

    loads[2].wait()
    loads[3].wait()
    for copy in sums + list(over.values()) + norms:
        copy.wait_recv()
    for copy in started:
        copy.wait_send()


def update(limit, total, squares, weights, mom, par, new_par_hbm, new_mom_hbm, prev_out_hbm, new_par, new_mom, store_sem):
    stores = [pltpu.make_async_copy(weights, prev_out_hbm, store_sem.at[0])]
    stores[0].start()
    norm = jnp.sum(jnp.sum(squares[...], axis=0), axis=1, keepdims=True)
    clip = jnp.minimum(jnp.float32(1.0), jnp.float32(limit) / jnp.sqrt(norm + jnp.float32(1e-06)))
    scaled = clip * total[...].astype(jnp.float32)
    fresh = momentum_coef * mom[...] + scaled
    new_mom[...] = fresh
    stores.append(pltpu.make_async_copy(new_mom, new_mom_hbm, store_sem.at[1]))
    stores[-1].start()
    new_par[...] = par[...] - outer_rate * (scaled + momentum_coef * fresh)
    stores.append(pltpu.make_async_copy(new_par, new_par_hbm, store_sem.at[2]))
    stores[-1].start()
    for copy in stores:
        copy.wait()


def by_kernel(sizes, replica_delta, momentum, params, prev_master):
    nz, nx, ns = sizes
    own, width = momentum.shape
    half, piece = width // ns, width // (ns * nx)
    b16, f32, dma = jnp.bfloat16, jnp.float32, pltpu.SemaphoreType.DMA
    delta = replica_delta.reshape(nz, own, width)
    hbm_space, vmem_space = (pl.BlockSpec(memory_space=m) for m in (pltpu.HBM, pltpu.VMEM))
    held = pl.pallas_call(
        functools.partial(exchange, sizes),
        out_shape=(
            pltpu.VMEM((own, width), b16),
            pltpu.VMEM((nz * nx * ns, 1, LANES), f32),
            pltpu.VMEM((nz, own, width), b16),
            pltpu.VMEM((own, width), f32),
            pltpu.VMEM((own, width), f32),
        ),
        in_specs=[hbm_space] * 4,
        out_specs=[vmem_space] * 5,
        scratch_shapes=[
            pltpu.VMEM((nz, own, width), b16),
            pltpu.VMEM((own, width), f32),
            pltpu.VMEM((nz, own, half), b16),
            pltpu.VMEM((nz, nx, own, piece), b16),
            pltpu.VMEM((nz, own, piece), f32),
            pltpu.VMEM((nz, nx, own, piece), b16),
            pltpu.VMEM((nz, own, piece), b16),
            pltpu.VMEM((nz, own, piece), b16),
            dma((4,)),
            dma((nz,)), dma((nz,)),
            dma((nz, nx)), dma((nz, nx)),
            dma((nz,)), dma((nz,)),
            dma((nx, ns)), dma((nx, ns)),
            dma((nz * nx * ns,)), dma((nz * nx * ns,)),
            dma((nz,)), dma((nz,)),
            dma((nz, nx)), dma((nz, nx)),
            dma((nz,)), dma((nz,)),
        ],
        compiler_params=pltpu.CompilerParams(
            collective_id=0, has_side_effects=True, vmem_limit_bytes=16 * 1024 * 1024
        ),
    )(*(pltpu.with_memory_space_constraint(a, pltpu.HBM) for a in (delta, momentum, params, prev_master)))
    new_params, new_momentum, weights = pl.pallas_call(
        functools.partial(update, math.sqrt(nz * own * width)),
        out_shape=(
            jax.ShapeDtypeStruct((own, width), f32),
            jax.ShapeDtypeStruct((own, width), f32),
            jax.ShapeDtypeStruct((nz, own, width), b16),
        ),
        in_specs=[vmem_space] * 5,
        out_specs=[hbm_space] * 3,
        scratch_shapes=[pltpu.VMEM((own, width), f32), pltpu.VMEM((own, width), f32), dma((3,))],
        compiler_params=pltpu.CompilerParams(vmem_limit_bytes=16 * 1024 * 1024),
    )(*held)
    return new_params, new_momentum, weights.reshape(nz * own, width)


def by_collectives(replica_delta, momentum, params, prev_master):
    own_delta = replica_delta[0]
    entries = own_delta.shape[0] * own_delta.shape[1]
    share_sum = lax.psum_scatter(own_delta, "blk", scatter_dimension=0, tiled=True)
    summed = lax.psum(share_sum, ("rep", "sub")).astype(jnp.float32)
    squares = lax.psum(jnp.sum(summed * summed), "blk")
    clip_factor = jnp.minimum(
        jnp.float32(1.0), jnp.sqrt(jnp.float32(entries)) / jnp.sqrt(squares + 1e-06)
    )
    scaled = clip_factor * summed
    new_momentum = momentum_coef * momentum + scaled
    new_params = params - outer_rate * (scaled + momentum_coef * new_momentum)
    prev_weights = lax.all_gather(prev_master.astype(jnp.bfloat16), "blk", axis=0, tiled=True)
    return (new_params, new_momentum, prev_weights)


def solution(mesh):
    sizes = tuple(mesh.shape[a] for a in ("blk", "rep", "sub"))

    def per_device(replica_delta, momentum, params, prev_master):
        width = momentum.shape[1]
        whole_pieces = width % (LANES * sizes[1] * sizes[2]) == 0
        powers = all(n & (n - 1) == 0 for n in sizes) and sizes[2] == 2
        if whole_pieces and powers:
            return by_kernel(sizes, replica_delta, momentum, params, prev_master)
        return by_collectives(replica_delta, momentum, params, prev_master)

    in_specs = (
        P(("groups", "blk", "rep", "sub"), None, None),
        P(("groups", "blk"), None),
        P(("groups", "blk"), None),
        P(("groups", "blk"), None),
    )
    out_specs = (P(("groups", "blk"), None), P(("groups", "blk"), None), P("groups", None))
    return jax.shard_map(
        per_device, mesh=mesh, in_specs=in_specs, out_specs=out_specs, check_vma=False
    )
```

```python
import functools
import itertools
import math

import jax
import jax.numpy as jnp
from jax import lax
from jax.experimental import pallas as pl
from jax.experimental.pallas import tpu as pltpu
from jax.sharding import PartitionSpec as P

momentum_coef = 0.9
outer_rate = 0.7
MESH = pl.DeviceIdType.MESH
LANES = 128


def flip(index, mask):
    bit = 1
    while bit <= mask:
        if mask & bit:
            index = index + bit * (1 - 2 * ((index // bit) % 2))
        bit *= 2
    return index


def exchange(sizes, delta_hbm, mom_hbm, par_hbm, prev_hbm, total, squares, weights, mom, par,
             delta, prev, recv1, half, mine, recv2, part, recv3,
             load_sem, send1, got1, send2, got2, send3, got3, send_g, got_g, send_q, got_q,
             send_pz, got_pz, send_px, got_px, send_pc, got_pc, round_sem):
    nz, nx, ns = sizes
    z, x, s = lax.axis_index("blk"), lax.axis_index("rep"), lax.axis_index("sub")
    own, width = mom.shape
    half_width = width // ns
    piece = half_width // nx

    def columns(core, rep):
        return pl.ds(pl.multiple_of(core * half_width + rep * piece, LANES), piece)

    def half_columns(core):
        return pl.ds(pl.multiple_of(core * half_width, LANES), half_width)

    def inner(rep):
        return pl.ds(pl.multiple_of(rep * piece, LANES), piece)

    def peer(tz, tx, ts):
        return {"blk": flip(z, tz), "rep": flip(x, tx), "sub": flip(s, ts)}

    def remote(src, dst, send, got, to):
        copy = pltpu.make_async_remote_copy(
            src_ref=src, dst_ref=dst, send_sem=send, recv_sem=got, device_id=peer(*to), device_id_type=MESH
        )
        copy.start()
        started.append(copy)
        return copy

    started = []
    offsets = [o for o in itertools.product(range(nz), range(nx), range(ns)) if o != (0, 0, 0)]
    barrier = pltpu.get_barrier_semaphore()
    around = (z > 0).astype(jnp.int32) + (z < nz - 1).astype(jnp.int32)

    def greet(semaphore):
        @pl.when(z > 0)
        def _():
            pl.semaphore_signal(semaphore, inc=1, device_id={"blk": z - 1}, device_id_type=MESH)

        @pl.when(z < nz - 1)
        def _():
            pl.semaphore_signal(semaphore, inc=1, device_id={"blk": z + 1}, device_id_type=MESH)

    greet(barrier)
    near = [(0, u, 0) for u in range(1, nx)] + [(0, 0, c) for c in range(1, ns)]
    for o in near:
        pl.semaphore_signal(barrier, inc=1, device_id=peer(*o), device_id_type=MESH)

    loads = [
        pltpu.make_async_copy(src, dst, load_sem.at[i])
        for i, (src, dst) in enumerate(((prev_hbm, prev), (delta_hbm, delta), (mom_hbm, mom), (par_hbm, par)))
    ]
    for copy in loads:
        copy.start()
    loads[0].wait()
    weights[z] = prev[...].astype(weights.dtype)
    loads[1].wait()
    pl.semaphore_wait(barrier, around + len(near))

    order = list(range(nz - 1, -1, -1))
    first = {
        t: remote(delta.at[flip(z, t), :, half_columns(1 - s)], recv1.at[t], send1.at[t], got1.at[t], (0, 0, 1))
        for t in order
    }
    second, third = {}, {}

    def stage_two(t):
        first[t].wait_recv()
        zt = flip(z, t)
        for u in range(nx - 1, 0, -1):
            xu = flip(x, u)
            half[t, u] = (
                delta[zt, :, columns(s, xu)].astype(jnp.float32) + recv1[t, :, inner(xu)].astype(jnp.float32)
            ).astype(half.dtype)
            second[t, u] = remote(half.at[t, u], recv2.at[t, u], send2.at[t, u], got2.at[t, u], (0, u, 0))
        mine[t] = delta[zt, :, columns(s, x)].astype(jnp.float32) + recv1[t, :, inner(x)].astype(jnp.float32)

    def stage_three(t):
        value = mine[t]
        for u in range(1, nx):
            second[t, u].wait_recv()
            value = value + recv2[t, u].astype(jnp.float32)
        if t:
            part[t] = value.astype(part.dtype)
            third[t] = remote(part.at[t], recv3.at[t], send3.at[t], got3.at[t], (t, 0, 0))
        else:
            mine[t] = value

    if nz > 2:
        greet(round_sem.at[0])
    stage_two(order[0])
    for r in range(nz - 2):
        pl.semaphore_wait(round_sem.at[r], around)
        if r + 1 < nz - 2:
            greet(round_sem.at[r + 1])
        if r == 0:
            stage_two(order[1])
    if nz == 2:
        stage_two(order[1])
    across = {
        t: remote(weights.at[z, :, columns(s, x)], weights.at[z, :, columns(s, x)], send_pz.at[t], got_pz.at[t], (t, 0, 0))
        for t in order if t
    }
    for i in range(1, nz):
        stage_three(order[i - 1])
        if i + 1 < nz:
            stage_two(order[i + 1])
    stage_three(order[-1])

    along = {}
    for t in order:
        if t:
            across[t].wait_recv()
            place = weights.at[flip(z, t), :, columns(s, x)]
            for u in range(1, nx):
                along[t, u] = remote(place, place, send_px.at[t, u], got_px.at[t, u], (0, u, 0))

    value = mine[0]
    for t in sorted(third):
        third[t].wait_recv()
        value = value + recv3[t].astype(jnp.float32)
    rounded = value.astype(total.dtype)
    total[:, columns(s, x)] = rounded
    value = rounded.astype(jnp.float32)
    square = jnp.sum(value * value, axis=0, keepdims=True)
    lanes = square[:, :LANES]
    for c in range(1, piece // LANES):
        lanes = lanes + square[:, c * LANES : (c + 1) * LANES]
    place = (z * nx + x) * ns + s
    squares[place] = lanes
    norms = [
        remote(squares.at[place], squares.at[place], send_q.at[i], got_q.at[i], o)
        for i, o in sorted(enumerate(offsets), key=lambda e: (-e[1][0], -e[1][1], -e[1][2]))
    ]
    sums = [
        remote(total.at[:, columns(s, x)], total.at[:, columns(s, x)], send_g.at[u, c], got_g.at[u, c], (0, u, c))
        for u in range(nx - 1, -1, -1) for c in range(ns - 1, -1, -1) if u or c
    ]

    over = {}
    for t in order:
        if t:
            for u in range(1, nx):
                along[t, u].wait_recv()
            place = weights.at[flip(z, t), :, half_columns(s)]
            over[t] = remote(place, place, send_pc.at[t], got_pc.at[t], (0, 0, 1))

    loads[2].wait()
    loads[3].wait()
    for copy in sums + list(over.values()) + norms:
        copy.wait_recv()
    for copy in started:
        copy.wait_send()


def update(limit, total, squares, weights, mom, par, new_par_hbm, new_mom_hbm, prev_out_hbm, new_par, new_mom, store_sem):
    stores = [pltpu.make_async_copy(weights, prev_out_hbm, store_sem.at[0])]
    stores[0].start()
    norm = jnp.sum(jnp.sum(squares[...], axis=0), axis=1, keepdims=True)
    clip = jnp.minimum(jnp.float32(1.0), jnp.float32(limit) / jnp.sqrt(norm + jnp.float32(1e-06)))
    scaled = clip * total[...].astype(jnp.float32)
    fresh = momentum_coef * mom[...] + scaled
    new_mom[...] = fresh
    stores.append(pltpu.make_async_copy(new_mom, new_mom_hbm, store_sem.at[1]))
    stores[-1].start()
    new_par[...] = par[...] - outer_rate * (scaled + momentum_coef * fresh)
    stores.append(pltpu.make_async_copy(new_par, new_par_hbm, store_sem.at[2]))
    stores[-1].start()
    for copy in stores:
        copy.wait()


def by_kernel(sizes, replica_delta, momentum, params, prev_master):
    nz, nx, ns = sizes
    own, width = momentum.shape
    half, piece = width // ns, width // (ns * nx)
    b16, f32, dma = jnp.bfloat16, jnp.float32, pltpu.SemaphoreType.DMA
    delta = replica_delta.reshape(nz, own, width)
    hbm_space, vmem_space = (pl.BlockSpec(memory_space=m) for m in (pltpu.HBM, pltpu.VMEM))
    held = pl.pallas_call(
        functools.partial(exchange, sizes),
        out_shape=(
            pltpu.VMEM((own, width), b16),
            pltpu.VMEM((nz * nx * ns, 1, LANES), f32),
            pltpu.VMEM((nz, own, width), b16),
            pltpu.VMEM((own, width), f32),
            pltpu.VMEM((own, width), f32),
        ),
        in_specs=[hbm_space] * 4,
        out_specs=[vmem_space] * 5,
        scratch_shapes=[
            pltpu.VMEM((nz, own, width), b16),
            pltpu.VMEM((own, width), f32),
            pltpu.VMEM((nz, own, half), b16),
            pltpu.VMEM((nz, nx, own, piece), b16),
            pltpu.VMEM((nz, own, piece), f32),
            pltpu.VMEM((nz, nx, own, piece), b16),
            pltpu.VMEM((nz, own, piece), b16),
            pltpu.VMEM((nz, own, piece), b16),
            dma((4,)),
            dma((nz,)), dma((nz,)),
            dma((nz, nx)), dma((nz, nx)),
            dma((nz,)), dma((nz,)),
            dma((nx, ns)), dma((nx, ns)),
            dma((nz * nx * ns,)), dma((nz * nx * ns,)),
            dma((nz,)), dma((nz,)),
            dma((nz, nx)), dma((nz, nx)),
            dma((nz,)), dma((nz,)),
            pltpu.SemaphoreType.REGULAR((max(nz - 2, 1),)),
        ],
        compiler_params=pltpu.CompilerParams(
            collective_id=0, has_side_effects=True, vmem_limit_bytes=16 * 1024 * 1024
        ),
    )(*(pltpu.with_memory_space_constraint(a, pltpu.HBM) for a in (delta, momentum, params, prev_master)))
    new_params, new_momentum, weights = pl.pallas_call(
        functools.partial(update, math.sqrt(nz * own * width)),
        out_shape=(
            jax.ShapeDtypeStruct((own, width), f32),
            jax.ShapeDtypeStruct((own, width), f32),
            jax.ShapeDtypeStruct((nz, own, width), b16),
        ),
        in_specs=[vmem_space] * 5,
        out_specs=[hbm_space] * 3,
        scratch_shapes=[pltpu.VMEM((own, width), f32), pltpu.VMEM((own, width), f32), dma((3,))],
        compiler_params=pltpu.CompilerParams(vmem_limit_bytes=16 * 1024 * 1024),
    )(*held)
    return new_params, new_momentum, weights.reshape(nz * own, width)


def by_collectives(replica_delta, momentum, params, prev_master):
    own_delta = replica_delta[0]
    entries = own_delta.shape[0] * own_delta.shape[1]
    share_sum = lax.psum_scatter(own_delta, "blk", scatter_dimension=0, tiled=True)
    summed = lax.psum(share_sum, ("rep", "sub")).astype(jnp.float32)
    squares = lax.psum(jnp.sum(summed * summed), "blk")
    clip_factor = jnp.minimum(
        jnp.float32(1.0), jnp.sqrt(jnp.float32(entries)) / jnp.sqrt(squares + 1e-06)
    )
    scaled = clip_factor * summed
    new_momentum = momentum_coef * momentum + scaled
    new_params = params - outer_rate * (scaled + momentum_coef * new_momentum)
    prev_weights = lax.all_gather(prev_master.astype(jnp.bfloat16), "blk", axis=0, tiled=True)
    return (new_params, new_momentum, prev_weights)


def solution(mesh):
    sizes = tuple(mesh.shape[a] for a in ("blk", "rep", "sub"))

    def per_device(replica_delta, momentum, params, prev_master):
        width = momentum.shape[1]
        whole_pieces = width % (LANES * sizes[1] * sizes[2]) == 0
        powers = all(n & (n - 1) == 0 and n > 1 for n in sizes) and sizes[2] == 2
        if whole_pieces and powers:
            return by_kernel(sizes, replica_delta, momentum, params, prev_master)
        return by_collectives(replica_delta, momentum, params, prev_master)

    in_specs = (
        P(("groups", "blk", "rep", "sub"), None, None),
        P(("groups", "blk"), None),
        P(("groups", "blk"), None),
        P(("groups", "blk"), None),
    )
    out_specs = (P(("groups", "blk"), None), P(("groups", "blk"), None), P("groups", None))
    return jax.shard_map(
        per_device, mesh=mesh, in_specs=in_specs, out_specs=out_specs, check_vma=False
    )
```

```python
import functools
import itertools
import math

import jax
import jax.numpy as jnp
from jax import lax
from jax.experimental import pallas as pl
from jax.experimental.pallas import tpu as pltpu
from jax.sharding import PartitionSpec as P

momentum_coef = 0.9
outer_rate = 0.7
MESH = pl.DeviceIdType.MESH
LANES = 128


def flip(index, mask):
    bit = 1
    while bit <= mask:
        if mask & bit:
            index = index + bit * (1 - 2 * ((index // bit) % 2))
        bit *= 2
    return index


def exchange(sizes, delta_hbm, mom_hbm, par_hbm, prev_hbm, total, squares, weights, mom, par,
             delta, prev, recv1, half, mine, recv2, part, recv3,
             load_sem, send1, got1, send2, got2, send3, got3, send_g, got_g, send_q, got_q,
             send_pz, got_pz, send_px, got_px, send_pc, got_pc, round_sem):
    nz, nx, ns = sizes
    z, x, s = lax.axis_index("blk"), lax.axis_index("rep"), lax.axis_index("sub")
    own, width = mom.shape
    half_width = width // ns
    piece = half_width // nx

    def columns(core, rep):
        return pl.ds(pl.multiple_of(core * half_width + rep * piece, LANES), piece)

    def half_columns(core):
        return pl.ds(pl.multiple_of(core * half_width, LANES), half_width)

    def inner(rep):
        return pl.ds(pl.multiple_of(rep * piece, LANES), piece)

    def peer(tz, tx, ts):
        return {"blk": flip(z, tz), "rep": flip(x, tx), "sub": flip(s, ts)}

    def remote(src, dst, send, got, to):
        copy = pltpu.make_async_remote_copy(
            src_ref=src, dst_ref=dst, send_sem=send, recv_sem=got, device_id=peer(*to), device_id_type=MESH
        )
        copy.start()
        started.append(copy)
        return copy

    started = []
    offsets = [o for o in itertools.product(range(nz), range(nx), range(ns)) if o != (0, 0, 0)]
    barrier = pltpu.get_barrier_semaphore()
    around = (z > 0).astype(jnp.int32) + (z < nz - 1).astype(jnp.int32)

    def greet(semaphore):
        @pl.when(z > 0)
        def _():
            pl.semaphore_signal(semaphore, inc=1, device_id={"blk": z - 1}, device_id_type=MESH)

        @pl.when(z < nz - 1)
        def _():
            pl.semaphore_signal(semaphore, inc=1, device_id={"blk": z + 1}, device_id_type=MESH)

    greet(barrier)
    near = [(0, u, 0) for u in range(1, nx)] + [(0, 0, c) for c in range(1, ns)]
    for o in near:
        pl.semaphore_signal(barrier, inc=1, device_id=peer(*o), device_id_type=MESH)

    loads = [
        pltpu.make_async_copy(src, dst, load_sem.at[i])
        for i, (src, dst) in enumerate(((prev_hbm, prev), (delta_hbm, delta), (mom_hbm, mom), (par_hbm, par)))
    ]
    for copy in loads:
        copy.start()
    loads[0].wait()
    weights[z] = prev[...].astype(weights.dtype)
    loads[1].wait()
    pl.semaphore_wait(barrier, around + len(near))

    order = list(range(nz - 1, -1, -1))
    first = {
        t: remote(delta.at[flip(z, t), :, half_columns(1 - s)], recv1.at[t], send1.at[t], got1.at[t], (0, 0, 1))
        for t in order
    }
    second, third = {}, {}

    def stage_two(t):
        first[t].wait_recv()
        zt = flip(z, t)
        for u in range(nx - 1, 0, -1):
            xu = flip(x, u)
            half[t, u] = (
                delta[zt, :, columns(s, xu)].astype(jnp.float32) + recv1[t, :, inner(xu)].astype(jnp.float32)
            ).astype(half.dtype)
            second[t, u] = remote(half.at[t, u], recv2.at[t, u], send2.at[t, u], got2.at[t, u], (0, u, 0))
        mine[t] = delta[zt, :, columns(s, x)].astype(jnp.float32) + recv1[t, :, inner(x)].astype(jnp.float32)

    def stage_three(t):
        value = mine[t]
        for u in range(1, nx):
            second[t, u].wait_recv()
            value = value + recv2[t, u].astype(jnp.float32)
        if t:
            part[t] = value.astype(part.dtype)
            third[t] = remote(part.at[t], recv3.at[t], send3.at[t], got3.at[t], (t, 0, 0))
        else:
            mine[t] = value

    across = {}

    def send_previous(t):
        place = weights.at[z, :, columns(s, x)]
        across[t] = remote(place, place, send_pz.at[t], got_pz.at[t], (t, 0, 0))

    if nz > 2:
        greet(round_sem.at[0])
    send_previous(1)
    for t in order:
        stage_two(t)
    for r in range(nz - 2):
        pl.semaphore_wait(round_sem.at[r], around)
        if r + 1 < nz - 2:
            greet(round_sem.at[r + 1])
        send_previous(r + 2)
    for t in order:
        stage_three(t)

    along, over = {}, []
    for t in range(1, nz):
        across[t].wait_recv()
        place = weights.at[flip(z, t), :, columns(s, x)]
        for u in range(1, nx):
            along[t, u] = remote(place, place, send_px.at[t, u], got_px.at[t, u], (0, u, 0))
        over.append(remote(place, place, send_pc.at[t, 0], got_pc.at[t, 0], (0, 0, 1)))

    value = mine[0]
    for t in sorted(third):
        third[t].wait_recv()
        value = value + recv3[t].astype(jnp.float32)
    rounded = value.astype(total.dtype)
    total[:, columns(s, x)] = rounded
    value = rounded.astype(jnp.float32)
    square = jnp.sum(value * value, axis=0, keepdims=True)
    lanes = square[:, :LANES]
    for c in range(1, piece // LANES):
        lanes = lanes + square[:, c * LANES : (c + 1) * LANES]
    place = (z * nx + x) * ns + s
    squares[place] = lanes
    norms = [
        remote(squares.at[place], squares.at[place], send_q.at[i], got_q.at[i], o)
        for i, o in sorted(enumerate(offsets), key=lambda e: (-e[1][0], -e[1][1], -e[1][2]))
    ]
    sums = [
        remote(total.at[:, columns(s, x)], total.at[:, columns(s, x)], send_g.at[u, c], got_g.at[u, c], (0, u, c))
        for u in range(nx - 1, -1, -1) for c in range(ns - 1, -1, -1) if u or c
    ]

    for (t, u), copy in along.items():
        copy.wait_recv()
        place = weights.at[flip(z, t), :, columns(s, flip(x, u))]
        over.append(remote(place, place, send_pc.at[t, u], got_pc.at[t, u], (0, 0, 1)))

    loads[2].wait()
    loads[3].wait()
    for copy in sums + over + norms:
        copy.wait_recv()
    for copy in started:
        copy.wait_send()


def update(limit, total, squares, weights, mom, par, new_par_hbm, new_mom_hbm, prev_out_hbm, new_par, new_mom, store_sem):
    stores = [pltpu.make_async_copy(weights, prev_out_hbm, store_sem.at[0])]
    stores[0].start()
    norm = jnp.sum(jnp.sum(squares[...], axis=0), axis=1, keepdims=True)
    clip = jnp.minimum(jnp.float32(1.0), jnp.float32(limit) / jnp.sqrt(norm + jnp.float32(1e-06)))
    scaled = clip * total[...].astype(jnp.float32)
    fresh = momentum_coef * mom[...] + scaled
    new_mom[...] = fresh
    stores.append(pltpu.make_async_copy(new_mom, new_mom_hbm, store_sem.at[1]))
    stores[-1].start()
    new_par[...] = par[...] - outer_rate * (scaled + momentum_coef * fresh)
    stores.append(pltpu.make_async_copy(new_par, new_par_hbm, store_sem.at[2]))
    stores[-1].start()
    for copy in stores:
        copy.wait()


def by_kernel(sizes, replica_delta, momentum, params, prev_master):
    nz, nx, ns = sizes
    own, width = momentum.shape
    half, piece = width // ns, width // (ns * nx)
    b16, f32, dma = jnp.bfloat16, jnp.float32, pltpu.SemaphoreType.DMA
    delta = replica_delta.reshape(nz, own, width)
    hbm_space, vmem_space = (pl.BlockSpec(memory_space=m) for m in (pltpu.HBM, pltpu.VMEM))
    held = pl.pallas_call(
        functools.partial(exchange, sizes),
        out_shape=(
            pltpu.VMEM((own, width), b16),
            pltpu.VMEM((nz * nx * ns, 1, LANES), f32),
            pltpu.VMEM((nz, own, width), b16),
            pltpu.VMEM((own, width), f32),
            pltpu.VMEM((own, width), f32),
        ),
        in_specs=[hbm_space] * 4,
        out_specs=[vmem_space] * 5,
        scratch_shapes=[
            pltpu.VMEM((nz, own, width), b16),
            pltpu.VMEM((own, width), f32),
            pltpu.VMEM((nz, own, half), b16),
            pltpu.VMEM((nz, nx, own, piece), b16),
            pltpu.VMEM((nz, own, piece), f32),
            pltpu.VMEM((nz, nx, own, piece), b16),
            pltpu.VMEM((nz, own, piece), b16),
            pltpu.VMEM((nz, own, piece), b16),
            dma((4,)),
            dma((nz,)), dma((nz,)),
            dma((nz, nx)), dma((nz, nx)),
            dma((nz,)), dma((nz,)),
            dma((nx, ns)), dma((nx, ns)),
            dma((nz * nx * ns,)), dma((nz * nx * ns,)),
            dma((nz,)), dma((nz,)),
            dma((nz, nx)), dma((nz, nx)),
            dma((nz, nx)), dma((nz, nx)),
            pltpu.SemaphoreType.REGULAR((max(nz - 2, 1),)),
        ],
        compiler_params=pltpu.CompilerParams(
            collective_id=0, has_side_effects=True, vmem_limit_bytes=16 * 1024 * 1024
        ),
    )(*(pltpu.with_memory_space_constraint(a, pltpu.HBM) for a in (delta, momentum, params, prev_master)))
    new_params, new_momentum, weights = pl.pallas_call(
        functools.partial(update, math.sqrt(nz * own * width)),
        out_shape=(
            jax.ShapeDtypeStruct((own, width), f32),
            jax.ShapeDtypeStruct((own, width), f32),
            jax.ShapeDtypeStruct((nz, own, width), b16),
        ),
        in_specs=[vmem_space] * 5,
        out_specs=[hbm_space] * 3,
        scratch_shapes=[pltpu.VMEM((own, width), f32), pltpu.VMEM((own, width), f32), dma((3,))],
        compiler_params=pltpu.CompilerParams(vmem_limit_bytes=16 * 1024 * 1024),
    )(*held)
    return new_params, new_momentum, weights.reshape(nz * own, width)


def by_collectives(replica_delta, momentum, params, prev_master):
    own_delta = replica_delta[0]
    entries = own_delta.shape[0] * own_delta.shape[1]
    share_sum = lax.psum_scatter(own_delta, "blk", scatter_dimension=0, tiled=True)
    summed = lax.psum(share_sum, ("rep", "sub")).astype(jnp.float32)
    squares = lax.psum(jnp.sum(summed * summed), "blk")
    clip_factor = jnp.minimum(
        jnp.float32(1.0), jnp.sqrt(jnp.float32(entries)) / jnp.sqrt(squares + 1e-06)
    )
    scaled = clip_factor * summed
    new_momentum = momentum_coef * momentum + scaled
    new_params = params - outer_rate * (scaled + momentum_coef * new_momentum)
    prev_weights = lax.all_gather(prev_master.astype(jnp.bfloat16), "blk", axis=0, tiled=True)
    return (new_params, new_momentum, prev_weights)


def solution(mesh):
    sizes = tuple(mesh.shape[a] for a in ("blk", "rep", "sub"))

    def per_device(replica_delta, momentum, params, prev_master):
        width = momentum.shape[1]
        whole_pieces = width % (LANES * sizes[1] * sizes[2]) == 0
        powers = all(n & (n - 1) == 0 and n > 1 for n in sizes) and sizes[2] == 2
        if whole_pieces and powers:
            return by_kernel(sizes, replica_delta, momentum, params, prev_master)
        return by_collectives(replica_delta, momentum, params, prev_master)

    in_specs = (
        P(("groups", "blk", "rep", "sub"), None, None),
        P(("groups", "blk"), None),
        P(("groups", "blk"), None),
        P(("groups", "blk"), None),
    )
    out_specs = (P(("groups", "blk"), None), P(("groups", "blk"), None), P("groups", None))
    return jax.shard_map(
        per_device, mesh=mesh, in_specs=in_specs, out_specs=out_specs, check_vma=False
    )
```

```python
import functools
import itertools
import math

import jax
import jax.numpy as jnp
from jax import lax
from jax.experimental import pallas as pl
from jax.experimental.pallas import tpu as pltpu
from jax.sharding import PartitionSpec as P

momentum_coef = 0.9
outer_rate = 0.7
MESH = pl.DeviceIdType.MESH
LANES = 128


def flip(index, mask):
    bit = 1
    while bit <= mask:
        if mask & bit:
            index = index + bit * (1 - 2 * ((index // bit) % 2))
        bit *= 2
    return index


def exchange(sizes, delta_hbm, mom_hbm, par_hbm, prev_hbm, total, squares, weights, mom, par,
             delta, prev, recv1, half, mine, recv2, part, recv3,
             load_sem, send1, got1, send2, got2, send3, got3, send_g, got_g, send_q, got_q,
             send_pz, got_pz, send_px, got_px, send_pc, got_pc, round_sem):
    nz, nx, ns = sizes
    z, x, s = lax.axis_index("blk"), lax.axis_index("rep"), lax.axis_index("sub")
    own, width = mom.shape
    half_width = width // ns
    piece = half_width // nx

    def columns(core, rep):
        return pl.ds(pl.multiple_of(core * half_width + rep * piece, LANES), piece)

    def half_columns(core):
        return pl.ds(pl.multiple_of(core * half_width, LANES), half_width)

    def inner(rep):
        return pl.ds(pl.multiple_of(rep * piece, LANES), piece)

    def peer(tz, tx, ts):
        return {"blk": flip(z, tz), "rep": flip(x, tx), "sub": flip(s, ts)}

    def remote(src, dst, send, got, to):
        copy = pltpu.make_async_remote_copy(
            src_ref=src, dst_ref=dst, send_sem=send, recv_sem=got, device_id=peer(*to), device_id_type=MESH
        )
        copy.start()
        started.append(copy)
        return copy

    started = []
    offsets = [o for o in itertools.product(range(nz), range(nx), range(ns)) if o != (0, 0, 0)]
    barrier = pltpu.get_barrier_semaphore()
    around = (z > 0).astype(jnp.int32) + (z < nz - 1).astype(jnp.int32)

    def greet(semaphore):
        @pl.when(z > 0)
        def _():
            pl.semaphore_signal(semaphore, inc=1, device_id={"blk": z - 1}, device_id_type=MESH)

        @pl.when(z < nz - 1)
        def _():
            pl.semaphore_signal(semaphore, inc=1, device_id={"blk": z + 1}, device_id_type=MESH)

    greet(barrier)
    near = [(0, u, 0) for u in range(1, nx)] + [(0, 0, c) for c in range(1, ns)]
    for o in near:
        pl.semaphore_signal(barrier, inc=1, device_id=peer(*o), device_id_type=MESH)

    loads = [
        pltpu.make_async_copy(src, dst, load_sem.at[i])
        for i, (src, dst) in enumerate(((delta_hbm, delta), (prev_hbm, prev), (mom_hbm, mom), (par_hbm, par)))
    ]
    for copy in loads:
        copy.start()
    loads[0].wait()
    pl.semaphore_wait(barrier, around + len(near))

    order = list(range(nz - 1, -1, -1))
    first = {
        t: remote(delta.at[flip(z, t), :, half_columns(1 - s)], recv1.at[t], send1.at[t], got1.at[t], (0, 0, 1))
        for t in order
    }
    second, third = {}, {}

    def stage_two(t):
        first[t].wait_recv()
        zt = flip(z, t)
        for u in range(nx - 1, 0, -1):
            xu = flip(x, u)
            half[t, u] = (
                delta[zt, :, columns(s, xu)].astype(jnp.float32) + recv1[t, :, inner(xu)].astype(jnp.float32)
            ).astype(half.dtype)
            second[t, u] = remote(half.at[t, u], recv2.at[t, u], send2.at[t, u], got2.at[t, u], (0, u, 0))
        mine[t] = delta[zt, :, columns(s, x)].astype(jnp.float32) + recv1[t, :, inner(x)].astype(jnp.float32)

    def stage_three(t):
        value = mine[t]
        for u in range(1, nx):
            second[t, u].wait_recv()
            value = value + recv2[t, u].astype(jnp.float32)
        if t:
            part[t] = value.astype(part.dtype)
            third[t] = remote(part.at[t], recv3.at[t], send3.at[t], got3.at[t], (t, 0, 0))
        else:
            mine[t] = value

    across = {}

    def send_previous(t):
        place = weights.at[z, :, columns(s, x)]
        across[t] = remote(place, place, send_pz.at[t], got_pz.at[t], (t, 0, 0))

    if nz > 2:
        greet(round_sem.at[0])
    loads[1].wait()
    weights[z] = prev[...].astype(weights.dtype)
    send_previous(1)
    for t in order:
        stage_two(t)
    for r in range(nz - 2):
        pl.semaphore_wait(round_sem.at[r], around)
        if r + 1 < nz - 2:
            greet(round_sem.at[r + 1])
        send_previous(r + 2)
    for t in order:
        stage_three(t)

    along, over = {}, []
    for t in range(1, nz):
        across[t].wait_recv()
        place = weights.at[flip(z, t), :, columns(s, x)]
        for u in range(1, nx):
            along[t, u] = remote(place, place, send_px.at[t, u], got_px.at[t, u], (0, u, 0))
        over.append(remote(place, place, send_pc.at[t, 0], got_pc.at[t, 0], (0, 0, 1)))

    value = mine[0]
    for t in sorted(third):
        third[t].wait_recv()
        value = value + recv3[t].astype(jnp.float32)
    rounded = value.astype(total.dtype)
    total[:, columns(s, x)] = rounded
    value = rounded.astype(jnp.float32)
    square = jnp.sum(value * value, axis=0, keepdims=True)
    lanes = square[:, :LANES]
    for c in range(1, piece // LANES):
        lanes = lanes + square[:, c * LANES : (c + 1) * LANES]
    place = (z * nx + x) * ns + s
    squares[place] = lanes
    norms = [
        remote(squares.at[place], squares.at[place], send_q.at[i], got_q.at[i], o)
        for i, o in sorted(enumerate(offsets), key=lambda e: (-e[1][0], -e[1][1], -e[1][2]))
    ]
    sums = [
        remote(total.at[:, columns(s, x)], total.at[:, columns(s, x)], send_g.at[u, c], got_g.at[u, c], (0, u, c))
        for u in range(nx - 1, -1, -1) for c in range(ns - 1, -1, -1) if u or c
    ]

    for (t, u), copy in along.items():
        copy.wait_recv()
        place = weights.at[flip(z, t), :, columns(s, flip(x, u))]
        over.append(remote(place, place, send_pc.at[t, u], got_pc.at[t, u], (0, 0, 1)))

    loads[2].wait()
    loads[3].wait()
    for copy in sums + over + norms:
        copy.wait_recv()
    for copy in started:
        copy.wait_send()


def update(limit, total, squares, weights, mom, par, new_par_hbm, new_mom_hbm, prev_out_hbm, new_par, new_mom, store_sem):
    stores = [pltpu.make_async_copy(weights, prev_out_hbm, store_sem.at[0])]
    stores[0].start()
    norm = jnp.sum(jnp.sum(squares[...], axis=0), axis=1, keepdims=True)
    clip = jnp.minimum(jnp.float32(1.0), jnp.float32(limit) / jnp.sqrt(norm + jnp.float32(1e-06)))
    scaled = clip * total[...].astype(jnp.float32)
    fresh = momentum_coef * mom[...] + scaled
    new_mom[...] = fresh
    stores.append(pltpu.make_async_copy(new_mom, new_mom_hbm, store_sem.at[1]))
    stores[-1].start()
    new_par[...] = par[...] - outer_rate * (scaled + momentum_coef * fresh)
    stores.append(pltpu.make_async_copy(new_par, new_par_hbm, store_sem.at[2]))
    stores[-1].start()
    for copy in stores:
        copy.wait()


def by_kernel(sizes, replica_delta, momentum, params, prev_master):
    nz, nx, ns = sizes
    own, width = momentum.shape
    half, piece = width // ns, width // (ns * nx)
    b16, f32, dma = jnp.bfloat16, jnp.float32, pltpu.SemaphoreType.DMA
    delta = replica_delta.reshape(nz, own, width)
    hbm_space, vmem_space = (pl.BlockSpec(memory_space=m) for m in (pltpu.HBM, pltpu.VMEM))
    held = pl.pallas_call(
        functools.partial(exchange, sizes),
        out_shape=(
            pltpu.VMEM((own, width), b16),
            pltpu.VMEM((nz * nx * ns, 1, LANES), f32),
            pltpu.VMEM((nz, own, width), b16),
            pltpu.VMEM((own, width), f32),
            pltpu.VMEM((own, width), f32),
        ),
        in_specs=[hbm_space] * 4,
        out_specs=[vmem_space] * 5,
        scratch_shapes=[
            pltpu.VMEM((nz, own, width), b16),
            pltpu.VMEM((own, width), f32),
            pltpu.VMEM((nz, own, half), b16),
            pltpu.VMEM((nz, nx, own, piece), b16),
            pltpu.VMEM((nz, own, piece), f32),
            pltpu.VMEM((nz, nx, own, piece), b16),
            pltpu.VMEM((nz, own, piece), b16),
            pltpu.VMEM((nz, own, piece), b16),
            dma((4,)),
            dma((nz,)), dma((nz,)),
            dma((nz, nx)), dma((nz, nx)),
            dma((nz,)), dma((nz,)),
            dma((nx, ns)), dma((nx, ns)),
            dma((nz * nx * ns,)), dma((nz * nx * ns,)),
            dma((nz,)), dma((nz,)),
            dma((nz, nx)), dma((nz, nx)),
            dma((nz, nx)), dma((nz, nx)),
            pltpu.SemaphoreType.REGULAR((max(nz - 2, 1),)),
        ],
        compiler_params=pltpu.CompilerParams(
            collective_id=0, has_side_effects=True, vmem_limit_bytes=16 * 1024 * 1024
        ),
    )(*(pltpu.with_memory_space_constraint(a, pltpu.HBM) for a in (delta, momentum, params, prev_master)))
    new_params, new_momentum, weights = pl.pallas_call(
        functools.partial(update, math.sqrt(nz * own * width)),
        out_shape=(
            jax.ShapeDtypeStruct((own, width), f32),
            jax.ShapeDtypeStruct((own, width), f32),
            jax.ShapeDtypeStruct((nz, own, width), b16),
        ),
        in_specs=[vmem_space] * 5,
        out_specs=[hbm_space] * 3,
        scratch_shapes=[pltpu.VMEM((own, width), f32), pltpu.VMEM((own, width), f32), dma((3,))],
        compiler_params=pltpu.CompilerParams(vmem_limit_bytes=16 * 1024 * 1024),
    )(*held)
    return new_params, new_momentum, weights.reshape(nz * own, width)


def by_collectives(replica_delta, momentum, params, prev_master):
    own_delta = replica_delta[0]
    entries = own_delta.shape[0] * own_delta.shape[1]
    share_sum = lax.psum_scatter(own_delta, "blk", scatter_dimension=0, tiled=True)
    summed = lax.psum(share_sum, ("rep", "sub")).astype(jnp.float32)
    squares = lax.psum(jnp.sum(summed * summed), "blk")
    clip_factor = jnp.minimum(
        jnp.float32(1.0), jnp.sqrt(jnp.float32(entries)) / jnp.sqrt(squares + 1e-06)
    )
    scaled = clip_factor * summed
    new_momentum = momentum_coef * momentum + scaled
    new_params = params - outer_rate * (scaled + momentum_coef * new_momentum)
    prev_weights = lax.all_gather(prev_master.astype(jnp.bfloat16), "blk", axis=0, tiled=True)
    return (new_params, new_momentum, prev_weights)


def solution(mesh):
    sizes = tuple(mesh.shape[a] for a in ("blk", "rep", "sub"))

    def per_device(replica_delta, momentum, params, prev_master):
        width = momentum.shape[1]
        whole_pieces = width % (LANES * sizes[1] * sizes[2]) == 0
        powers = all(n & (n - 1) == 0 and n > 1 for n in sizes) and sizes[2] == 2
        if whole_pieces and powers:
            return by_kernel(sizes, replica_delta, momentum, params, prev_master)
        return by_collectives(replica_delta, momentum, params, prev_master)

    in_specs = (
        P(("groups", "blk", "rep", "sub"), None, None),
        P(("groups", "blk"), None),
        P(("groups", "blk"), None),
        P(("groups", "blk"), None),
    )
    out_specs = (P(("groups", "blk"), None), P(("groups", "blk"), None), P("groups", None))
    return jax.shard_map(
        per_device, mesh=mesh, in_specs=in_specs, out_specs=out_specs, check_vma=False
    )
```
